1024 devices in a mesh: occ: 64 (over x, z), vir: 16 (over y, core).
Axes of the slice: x: 4, y: 8, z: 16, core: 2. Of those that a mesh axis runs over, the one named last changes fastest.
Arguments:
- amps: float32 [8192, 16, 1024], P('occ', 'vir'), may hold values from -6 to 6
- resid: float32 [8192, 16, 1024], P('occ', 'vir'), may hold values from -6 to 6
- ints: float32 [16, 1024, 1024], P('vir', 'occ'), may hold values from -0.5 to 0.5
- tasks: int32 [16], replicated, may hold values from 0 to 15
- pair_tiles: int32 [16, 2], replicated, may hold values from 0 to 18
- irreps: int32 [19, 32], replicated, may hold values from 0 to 7
Outputs:
- updated: float32 [8192, 16, 1024], P('occ', 'vir')
The draws below stay inside these ranges and needn't reach their ends.
All inputs are finite; a program needn't handle non-finite values.
Results may differ from the reference program's by a relative error of at most 0.0003.
Values sent between devices are 32-bit elements; how exact they have to be, the bound alone decides.
A program may use at most 32 MiB of HBM per device.

```python
import jax
import jax.numpy as jnp
from jax import lax

TILE = 32
NVT = 19
PT = 1024
NPT = 16
O2 = 8192


def touch_ends(result, stream_key, least, top_value):
    dims = result.shape
    spot = [jax.random.randint(jax.random.fold_in(stream_key, axis), (), 0, dims[axis]) for axis in range(len(dims))]
    result = result.at[tuple(spot)].set(least)
    longest = dims.index(max(dims))
    spot[longest] = (spot[longest] + 1) % dims[longest]
    return result.at[tuple(spot)].set(top_value)


def steps_of(stream_key, dims, cuts, smallest, largest):
    factor_of, own = 1.0, jax.random.fold_in(stream_key, 6)
    for position, parts in cuts:
        heights = jnp.exp(jax.random.uniform(jax.random.fold_in(own, position), (parts,), jnp.float32, smallest / len(cuts), largest / len(cuts)))
        factor_of = factor_of * jnp.repeat(heights, dims[position] // parts).reshape([-1 if axis == position else 1 for axis in range(len(dims))])
    return factor_of


def normal_values(rng, extent, spread, bound, cuts=(), kind=jnp.bfloat16):
    loudness = steps_of(rng, extent, cuts, -0.22, 0.18) if cuts else 1.0
    array = jax.random.normal(rng, extent, jnp.float32) * spread * loudness
    return jnp.minimum(jnp.maximum(array, -bound), bound).astype(kind)


def setup_inputs(seed: int = 0) -> dict:
    key_list = jax.random.split(jax.random.key(seed), 7)
    amps = normal_values(key_list[0], (O2, NPT, PT), 1.0, 6.0, ((0, 64), (1, 16)), jnp.float32)
    resid = normal_values(key_list[1], (O2, NPT, PT), 1.0, 6.0, ((0, 64), (1, 16)), jnp.float32)
    ints = normal_values(key_list[2], (NPT, PT, PT), (PT // 8) ** -0.5, 0.5, ((0, 16), (1, 64)), jnp.float32)
    tasks = touch_ends(jax.random.randint(key_list[3], (NPT,), 0, NPT), jax.random.fold_in(key_list[3], 1), 0, NPT - 1).astype(jnp.int32)
    pair_tiles = touch_ends(jax.random.randint(key_list[4], (NPT, 2), 0, NVT), jax.random.fold_in(key_list[4], 1), 0, NVT - 1).astype(jnp.int32)
    irreps = touch_ends(jax.random.randint(key_list[5], (NVT, TILE), 0, 8), jax.random.fold_in(key_list[5], 1), 0, 7).astype(jnp.int32)
    return dict(amps=amps, resid=resid, ints=ints, tasks=tasks, pair_tiles=pair_tiles, irreps=irreps)


def pair_irreps(tile_pair, irreps):
    first_row = irreps[tile_pair[0]]
    second_row = irreps[tile_pair[1]]
    return jnp.bitwise_xor(first_row[:, None], second_row[None, :]).reshape(-1)


def reference(amps, resid, ints, tasks, pair_tiles, irreps):
    def ladder_tile(task_index):
        cd_tile = tasks[task_index]
        selected = lax.dynamic_index_in_dim(amps, cd_tile, 1, keepdims=False)
        ab_irrep = pair_irreps(pair_tiles[task_index], irreps)
        cd_irrep = pair_irreps(pair_tiles[cd_tile], irreps)
        effective = jnp.where(ab_irrep[:, None] == cd_irrep[None, :], ints[task_index], jnp.zeros((), ints.dtype))
        return lax.dot_general(selected, effective, (((1,), (1,)), ((), ())), precision=lax.Precision.HIGHEST, preferred_element_type=jnp.float32)
    ladder = lax.map(ladder_tile, jnp.arange(NPT, dtype=jnp.int32))
    return resid + jnp.transpose(ladder, (1, 0, 2))
```

```python
import jax
import jax.numpy as jnp
from jax import lax
from jax.experimental import pallas as pl
from jax.experimental.pallas import tpu as pltpu
from jax.sharding import PartitionSpec as P

MESH = pl.DeviceIdType.MESH
X, Z, V = 4, 16, 16
SHARDS = X * Z
ROWS = 16
TILE = 32
COLS = 1024
BLOCKS = COLS // 128
NA = 3
WA = NA * 128
WB = COLS - WA
OCC = 128
SHARE = OCC // V
HALF = COLS // 2
FWD, BWD = Z // 2, Z // 2 - 1


def kernel(
    tasks, pairs, irr, amps, resid, ints, out,
    raw, ehi, elo, whole, sent0, sent1, spread0, spread1, picked, abuf, aa, base, col_key, cd_key,
    s_loc, s_a, s_b, s_y, r_ax, r_af, r_ab, r_bf, r_bb, r_bx, r_y1, r_y2,
):
    occ, vir = lax.axis_index("occ"), lax.axis_index("vir")
    x, z = occ // Z, occ % Z
    sign = 1 - 2 * (vir % 2)
    xf, xb = (x + sign + X) % X, (x - sign + X) % X
    xo = (x + 2) % X
    zf, zb = (z + sign + Z) % Z, (z - sign + Z) % Z
    to_xf, to_xb = (xf * Z + z, vir), (xb * Z + z, vir)
    to_zf, to_zb = (x * Z + zf, vir), (x * Z + zb, vir)

    load_amps = pltpu.make_async_copy(amps, whole, s_loc.at[1])
    load_amps.start()
    load_ints = pltpu.make_async_copy(ints, raw.at[occ], s_loc.at[0])
    load_ints.start()
    load_resid = pltpu.make_async_copy(resid, base, s_loc.at[2])
    load_resid.start()

    barrier = pltpu.get_barrier_semaphore()
    for who in (to_xf, to_xb, to_zf, to_zb):
        pl.semaphore_signal(barrier, inc=1, device_id=who, device_id_type=MESH)

    def greet(m, _):
        pl.semaphore_signal(barrier, inc=1, device_id=(occ, (vir + m) % V), device_id_type=MESH)
        return 0

    lax.fori_loop(1, V, greet, 0)

    tile_a, tile_b = pairs[0, vir], pairs[1, vir]
    task = tasks[vir]
    cd_a, cd_b = pairs[0, task], pairs[1, task]
    sub = lax.broadcasted_iota(jnp.int32, (ROWS, 128), 0)
    for par in range(2):
        key = jnp.zeros((ROWS, 128), jnp.int32)
        for j in range(ROWS):
            key = jnp.where(sub == j, irr[tile_b, par * ROWS + j], key)
        col_key[par] = key
    lane = lax.broadcasted_iota(jnp.int32, (1, 128), 1)
    minor = jnp.zeros((1, 128), jnp.int32)
    for j in range(TILE):
        minor = jnp.where(lane % TILE == j, irr[cd_b, j], minor)
    for b in range(BLOCKS):
        major = jnp.zeros((1, 128), jnp.int32)
        for j in range(4):
            major = jnp.where(lane // TILE == j, irr[cd_a, 4 * b + j], major)
        cd_key[:, 128 * b : 128 * b + 128] = major ^ minor

    sent, spread = (sent0, sent1), (spread0, spread1)
    load_amps.wait()

    def arrange(j, _):
        for b in range(BLOCKS):
            block = whole[pl.ds(SHARE * BLOCKS * j + b, SHARE, stride=BLOCKS), :]
            col = 128 * b % HALF
            sent[128 * b // HALF][j, :, col : col + 128] = block
        return 0

    lax.fori_loop(0, V, arrange, 0)
    load_ints.wait()
    pl.semaphore_wait(barrier, V + 3)

    def peer_at(i):
        return (vir + V // 2 + ((i + 1) // 2) * (1 - 2 * (i % 2)) + V) % V

    def spread_half(h):
        def send(i, _):
            peer = peer_at(i)
            pltpu.make_async_remote_copy(
                sent[h].at[peer], spread[h].at[vir],
                s_y.at[0, h], r_y1.at[h], device_id=(occ, peer), device_id_type=MESH,
            ).start()
            return 0

        lax.fori_loop(0, V - 1, send, 0)

    own_rows = pl.ds(pl.multiple_of(SHARE * vir, SHARE), SHARE)

    def return_half(h):
        many = spread[h].at[pl.ds(0, V - 1)]
        pltpu.make_async_copy(many, many, r_y1.at[h]).wait()
        for k in range(V):
            picked[h, k] = spread[h][tasks[k]]
        abuf[h, own_rows] = picked[h, vir]

        def send(i, _):
            peer = peer_at(i)
            pltpu.make_async_remote_copy(
                picked.at[h, peer], abuf.at[h, own_rows],
                s_y.at[1, h], r_y2.at[h], device_id=(occ, peer), device_id_type=MESH,
            ).start()
            return 0

        lax.fori_loop(0, V - 1, send, 0)

    def a_part(xx, zz):
        return raw.at[xx * Z + zz, :, pl.ds(0, WA)]

    def b_part(xx, zz):
        return raw.at[xx * Z + zz, :, pl.ds(WA, WB)]

    def push(part, send_sem, recv_sem, who):
        return pltpu.make_async_remote_copy(
            part, part, send_sem, recv_sem, device_id=who, device_id_type=MESH
        )

    def a_push(xx, zz, recv_sem, who):
        push(a_part(xx, zz), s_a.at[0], recv_sem, who).start()

    def b_push(xx, zz, recv_sem, who):
        push(b_part(xx, zz), s_b.at[0], recv_sem, who).start()

    def a_wait(xx, zz, recv_sem):
        push(a_part(xx, zz), s_a.at[0], recv_sem, to_xf).wait_recv()

    def b_wait(xx, zz, recv_sem):
        push(b_part(xx, zz), s_b.at[0], recv_sem, to_xf).wait_recv()

    xs = (x, xb, xf, xo)

    def prepare(xx, zz, first, last):
        shard = xx * Z + zz
        key = col_key[shard % 2] ^ irr[tile_a, shard // 2]
        rows = pl.ds(pl.multiple_of(shard * ROWS, ROWS), ROWS)
        cols = slice(128 * first, 128 * last)
        keys = jnp.concatenate([key] * (last - first), axis=1)
        value = jnp.where(keys == cd_key[:, cols], raw[shard, :, cols], 0.0)
        high = value.astype(jnp.bfloat16)
        ehi[rows, cols] = high
        elo[rows, cols] = (value - high.astype(jnp.float32)).astype(jnp.bfloat16)

    b_push(x, z, r_bf.at[0], to_zf)
    b_push(x, z, r_bb.at[0], to_zb)
    a_push(x, z, r_ax.at[0], to_xf)
    a_push(x, z, r_ax.at[1], to_xb)
    a_push(x, z, r_af.at[0, 0], to_zf)
    a_push(x, z, r_ab.at[0, 0], to_zb)
    b_push(x, z, r_bx.at[0, 0], to_xf)
    b_push(x, z, r_bx.at[1, 0], to_xb)
    spread_half(0)
    spread_half(1)
    for h in range(2):
        spread[h][vir] = sent[h][vir]

    a_wait(xb, z, r_ax.at[0])
    a_push(xb, z, r_ax.at[2], to_xf)
    a_push(xb, z, r_af.at[0, 1], to_zf)
    a_push(xb, z, r_ab.at[0, 1], to_zb)
    a_wait(xf, z, r_ax.at[1])
    a_push(xf, z, r_af.at[0, 2], to_zf)
    a_push(xf, z, r_ab.at[0, 2], to_zb)
    b_wait(xb, z, r_bx.at[0, 0])
    b_push(xb, z, r_bx.at[2, 0], to_xf)
    prepare(x, z, 0, BLOCKS)
    prepare(xb, z, 0, BLOCKS)
    a_wait(xo, z, r_ax.at[2])
    a_push(xo, z, r_af.at[0, 3], to_zf)
    a_push(xo, z, r_ab.at[0, 3], to_zb)

    def own_rest():
        b_wait(xf, z, r_bx.at[1, 0])
        prepare(xf, z, 0, BLOCKS)
        b_wait(xo, z, r_bx.at[2, 0])
        prepare(xo, z, 0, BLOCKS)

    def ways(s):
        yield (z - sign * (s + 1) + Z) % Z, r_af, r_bf, s + 1, FWD, to_zf
        yield (z + sign * (s + 1) + Z) % Z, r_ab, r_bb, s + 1 + FWD, BWD, to_zb

    def both(s, last=False):
        return list(ways(s))[: 1 if last else 2]

    def ring(s, final=0):
        way = both(s, final == 2)
        goes = (final < 2, final < 1)
        for (zz, r_a, r_b, q, _, to), go in zip(way, goes):
            b_wait(x, zz, r_b.at[s])
            if go:
                b_push(x, zz, r_b.at[s + 1], to)
            b_push(x, zz, r_bx.at[0, q], to_xf)
            b_push(x, zz, r_bx.at[1, q], to_xb)
        for i in range(X):
            for (zz, r_a, r_b, q, _, to), go in zip(way, goes):
                a_wait(xs[i], zz, r_a.at[s, i])
                if go:
                    a_push(xs[i], zz, r_a.at[s + 1, i], to)

    def settle(s, last=False):
        for zz, *_ in both(s, last):
            prepare(x, zz, 0, BLOCKS)
            for i in range(1, X):
                prepare(xs[i], zz, 0, NA)

    def pass_on(s, last=False):
        for zz, _, _, q, _, _ in both(s, last):
            b_wait(xb, zz, r_bx.at[0, q])
            b_push(xb, zz, r_bx.at[2, q], to_xf)

    def near(s, last=False):
        for zz, _, _, q, _, _ in both(s, last):
            prepare(xb, zz, NA, BLOCKS)
            b_wait(xf, zz, r_bx.at[1, q])
            prepare(xf, zz, NA, BLOCKS)

    def far(s, last=False):
        for zz, _, _, q, _, _ in both(s, last):
            b_wait(xo, zz, r_bx.at[2, q])
            prepare(xo, zz, NA, BLOCKS)

    def step(s, final=0):
        ring(s, final)
        pass_on(s - 1)
        settle(s, final == 2)
        near(s - 1)
        far(s - 2)

    def gather_amps(h):
        many = spread[h].at[pl.ds(0, V - 1)]
        pltpu.make_async_copy(many, many, r_y2.at[h]).wait()
        value = abuf[h]
        high = value.astype(jnp.bfloat16)
        cols = slice(HALF * h, HALF * h + HALF)
        aa[:OCC, cols] = high
        aa[OCC:, cols] = (value - high.astype(jnp.float32)).astype(jnp.bfloat16)

    def multiply(xx):
        span = Z * ROWS
        rows = pl.ds(pl.multiple_of(xx * span, span), span)
        right = aa[...]
        dims = (((1,), (1,)), ((), ()))
        part = lax.dot_general(ehi[rows, :], right, dims, preferred_element_type=jnp.float32)
        part += lax.dot_general(elo[rows, :], right, dims, preferred_element_type=jnp.float32)
        ladder = part[:, :OCC] + part[:, OCC:]
        for b in range(span // 128):
            here = pl.ds(xx * (span // 128) + b, OCC, stride=BLOCKS)
            out[here, :] = base[here, :] + ladder[128 * b : 128 * b + 128].T

    ring(0)
    own_rest()
    settle(0)
    ring(1)
    pass_on(0)
    settle(1)
    near(0)
    step(2)
    return_half(0)

    def body(s, _):
        step(s)
        return 0

    lax.fori_loop(3, 5, body, 0)
    return_half(1)
    step(5)
    step(6, 1)
    gather_amps(0)
    step(7, 2)
    pass_on(7, True)
    gather_amps(1)
    load_resid.wait()
    multiply(x)
    near(7, True)
    far(6)
    multiply(xb)
    multiply(xf)
    far(7, True)
    multiply(xo)

    a_all = raw.at[pl.ds(0, SHARDS - 1), :, pl.ds(0, WA)]
    pltpu.make_async_copy(a_all, a_all, s_a.at[0]).wait()
    b_all = raw.at[pl.ds(0, SHARDS - 1), :, pl.ds(WA, WB)]
    pltpu.make_async_copy(b_all, b_all, s_b.at[0]).wait()
    for phase in range(2):
        for h in range(2):
            many = spread[h].at[pl.ds(0, V - 1)]
            pltpu.make_async_copy(many, many, s_y.at[phase, h]).wait()


def solution(mesh):
    def shards(amps, resid, ints, tasks, pair_tiles, irreps):
        smem = pl.BlockSpec(memory_space=pltpu.SMEM)
        hbm = pl.BlockSpec(memory_space=pl.ANY)
        dma = pltpu.SemaphoreType.DMA
        f32, bf16 = jnp.float32, jnp.bfloat16
        flat = (OCC * BLOCKS, 128)
        total = pl.pallas_call(
            kernel,
            out_shape=jax.ShapeDtypeStruct(flat, f32),
            in_specs=[smem, smem, smem, hbm, hbm, hbm],
            out_specs=pl.BlockSpec(memory_space=pltpu.VMEM),
            scratch_shapes=[
                pltpu.VMEM((SHARDS, ROWS, COLS), f32),
                pltpu.VMEM((COLS, COLS), bf16),
                pltpu.VMEM((COLS, COLS), bf16),
                pltpu.VMEM(flat, f32),
                pltpu.VMEM((V, SHARE, HALF), f32),
                pltpu.VMEM((V, SHARE, HALF), f32),
                pltpu.VMEM((V, SHARE, HALF), f32),
                pltpu.VMEM((V, SHARE, HALF), f32),
                pltpu.VMEM((2, V, SHARE, HALF), f32),
                pltpu.VMEM((2, OCC, HALF), f32),
                pltpu.VMEM((2 * OCC, COLS), bf16),
                pltpu.VMEM(flat, f32),
                pltpu.VMEM((2, ROWS, 128), jnp.int32),
                pltpu.VMEM((1, COLS), jnp.int32),
                dma((3,)),
                dma((1,)),
                dma((1,)),
                dma((2, 2)),
                dma((3,)),
                dma((FWD, X)),
                dma((BWD, X)),
                dma((FWD,)),
                dma((BWD,)),
                dma((3, Z)),
                dma((2,)),
                dma((2,)),
            ],
            compiler_params=pltpu.CompilerParams(collective_id=0, has_side_effects=True),
            name="ladder",
        )(tasks, pair_tiles.T, irreps, amps.reshape(flat), resid.reshape(flat), ints.reshape(ROWS, COLS))
        return total.reshape(OCC, 1, COLS)

    in_specs = (P("occ", "vir", None), P("occ", "vir", None), P("vir", "occ", None), P(), P(), P())
    return jax.shard_map(
        shards, mesh=mesh, in_specs=in_specs, out_specs=P("occ", "vir", None), check_vma=False
    )
```

```python
import jax
import jax.numpy as jnp
from jax import lax
from jax.experimental import pallas as pl
from jax.experimental.pallas import tpu as pltpu
from jax.sharding import PartitionSpec as P

MESH = pl.DeviceIdType.MESH
X, Z, V = 4, 16, 16
SHARDS = X * Z
ROWS = 16
TILE = 32
COLS = 1024
BLOCKS = COLS // 128
NA = 2
WA = NA * 128
WB = COLS - WA
OCC = 128
SHARE = OCC // V
HALF = COLS // 2
FWD, BWD = Z // 2, Z // 2 - 1
HUB = V // 2


def kernel(
    tasks, pairs, irr, amps, resid, ints, out,
    raw, ehi, elo, whole, sent0, sent1, spread0, spread1, picked, abuf, aa, base, col_key, cd_key,
    s_loc, s_a, s_b, s_y, r_ax, r_af, r_ab, r_bf, r_bb, r_bx, r_y1, r_y2,
):
    occ, vir = lax.axis_index("occ"), lax.axis_index("vir")
    x, z = occ // Z, occ % Z
    sign = 1 - 2 * (vir % 2)
    xf, xb = (x + sign + X) % X, (x - sign + X) % X
    xo = (x + 2) % X
    zf, zb = (z + sign + Z) % Z, (z - sign + Z) % Z
    to_xf, to_xb = (xf * Z + z, vir), (xb * Z + z, vir)
    to_zf, to_zb = (x * Z + zf, vir), (x * Z + zb, vir)
    to_zf2 = (x * Z + (z + 2 * sign + Z) % Z, vir)
    to_zb2 = (x * Z + (z - 2 * sign + Z) % Z, vir)

    sent, spread = (sent0, sent1), (spread0, spread1)
    load_amps = pltpu.make_async_copy(amps, whole, s_loc.at[1])
    load_amps.start()
    load_ints = pltpu.make_async_copy(ints, raw.at[occ], s_loc.at[0])
    load_ints.start()
    load_resid = pltpu.make_async_copy(resid, base, s_loc.at[2])
    load_resid.start()

    barrier = pltpu.get_barrier_semaphore()
    for who in (to_xf, to_xb, to_zf, to_zb, to_zf2, to_zb2):
        pl.semaphore_signal(barrier, inc=1, device_id=who, device_id_type=MESH)

    is_hub = vir == HUB

    @pl.when(is_hub)
    def _():
        pl.semaphore_wait(barrier, 6 + V - 1)

        def tell(m, _):
            peer = (occ, (vir + m) % V)
            pl.semaphore_signal(barrier, inc=1, device_id=peer, device_id_type=MESH)
            return 0

        lax.fori_loop(1, V, tell, 0)

    @pl.when(jnp.logical_not(is_hub))
    def _():
        pl.semaphore_wait(barrier, 6)
        pl.semaphore_signal(barrier, inc=1, device_id=(occ, HUB), device_id_type=MESH)

    load_ints.wait()

    def peer_at(i):
        return (vir + V // 2 + ((i + 1) // 2) * (1 - 2 * (i % 2)) + V) % V

    def spread_half(h):
        def send(i, _):
            peer = peer_at(i)
            pltpu.make_async_remote_copy(
                sent[h].at[peer], spread[h].at[vir],
                s_y.at[0, h], r_y1.at[h], device_id=(occ, peer), device_id_type=MESH,
            ).start()
            return 0

        lax.fori_loop(0, V - 1, send, 0)

    own_rows = pl.ds(pl.multiple_of(SHARE * vir, SHARE), SHARE)

    def return_half(h):
        many = spread[h].at[pl.ds(0, V - 1)]
        pltpu.make_async_copy(many, many, r_y1.at[h]).wait()
        for k in range(V):
            picked[h, k] = spread[h][tasks[k]]
        abuf[h, own_rows] = picked[h, vir]

        def send(i, _):
            peer = peer_at(i)
            pltpu.make_async_remote_copy(
                picked.at[h, peer], abuf.at[h, own_rows],
                s_y.at[1, h], r_y2.at[h], device_id=(occ, peer), device_id_type=MESH,
            ).start()
            return 0

        lax.fori_loop(0, V - 1, send, 0)

    def a_part(xx, zz):
        return raw.at[xx * Z + zz, :, pl.ds(0, WA)]

    def b_part(xx, zz):
        return raw.at[xx * Z + zz, :, pl.ds(WA, WB)]

    def push(part, send_sem, recv_sem, who):
        return pltpu.make_async_remote_copy(
            part, part, send_sem, recv_sem, device_id=who, device_id_type=MESH
        )

    def a_push(xx, zz, recv_sem, who):
        push(a_part(xx, zz), s_a.at[0], recv_sem, who).start()

    def b_push(xx, zz, recv_sem, who):
        push(b_part(xx, zz), s_b.at[0], recv_sem, who).start()

    def a_wait(xx, zz, recv_sem):
        push(a_part(xx, zz), s_a.at[0], recv_sem, to_xf).wait_recv()

    def b_wait(xx, zz, recv_sem):
        push(b_part(xx, zz), s_b.at[0], recv_sem, to_xf).wait_recv()

    xs = (x, xb, xf, xo)

    def prepare(xx, zz, first, last):
        shard = xx * Z + zz
        key = col_key[shard % 2] ^ irr[tile_a, shard // 2]
        rows = pl.ds(pl.multiple_of(shard * ROWS, ROWS), ROWS)
        cols = slice(128 * first, 128 * last)
        keys = jnp.concatenate([key] * (last - first), axis=1)
        value = jnp.where(keys == cd_key[:, cols], raw[shard, :, cols], 0.0)
        high = value.astype(jnp.bfloat16)
        ehi[rows, cols] = high
        elo[rows, cols] = (value - high.astype(jnp.float32)).astype(jnp.bfloat16)

    ways = (
        (sign, FWD, r_af, r_bf, 0, to_zf, to_zf2),
        (-sign, BWD, r_ab, r_bb, FWD, to_zb, to_zb2),
    )

    def along(t):
        for d in (2 * t + 2, 2 * t + 1):
            for way in ways:
                if d <= way[1]:
                    yield d, (z - way[0] * d + Z) % Z, way

    def a_relay(i, d, zz, way):
        _, reach, r_a, _, _, to1, to2 = way
        if d + 2 <= reach:
            a_push(xs[i], zz, r_a.at[d + 1, i], to2)
        if d + 1 <= reach:
            a_push(xs[i], zz, r_a.at[d, i], to1)

    def b_relay(d, zz, way):
        _, reach, _, r_b, _, to1, to2 = way
        if d + 2 <= reach:
            b_push(x, zz, r_b.at[d + 1], to2)
        if d + 1 <= reach:
            b_push(x, zz, r_b.at[d], to1)

    def a_start(i):
        for way in ways:
            a_relay(i, 0, z, way)

    def stage_b(t):
        for d, zz, way in along(t):
            b_wait(x, zz, way[3].at[d - 1])
            if d % 2 == 0:
                b_relay(d, zz, way)
            b_push(x, zz, r_bx.at[0, way[4] + d], to_xf)
            b_push(x, zz, r_bx.at[1, way[4] + d], to_xb)

    def stage_a(t, i):
        for d, zz, way in along(t):
            if d % 2 == 0:
                a_wait(xs[i], zz, way[2].at[d - 1, i])
                a_relay(i, d, zz, way)

    def settle_a(t, i):
        for d, zz, way in along(t):
            if d % 2 == 1:
                a_wait(xs[i], zz, way[2].at[d - 1, i])
            prepare(xs[i], zz, 0, NA)

    def settle_b(t):
        for d, zz, way in along(t):
            prepare(x, zz, NA, BLOCKS)

    def pass_on(t):
        for d, zz, way in along(t):
            q = way[4] + d
            if d % 2 == 0:
                b_wait(xb, zz, r_bx.at[0, q])
                b_push(xb, zz, r_bx.at[2, q], to_xf)
            else:
                b_wait(xf, zz, r_bx.at[1, q])
                b_push(xf, zz, r_bx.at[2, q], to_xb)

    def near(t):
        for d, zz, way in along(t):
            q = way[4] + d
            if d % 2 == 0:
                b_wait(xf, zz, r_bx.at[1, q])
            else:
                b_wait(xb, zz, r_bx.at[0, q])
            prepare(xb, zz, NA, BLOCKS)
            prepare(xf, zz, NA, BLOCKS)

    def far(t):
        for d, zz, way in along(t):
            q = way[4] + d
            b_wait(xo, zz, r_bx.at[2, q])
            prepare(xo, zz, NA, BLOCKS)

    for way in ways:
        b_relay(0, z, way)
    a_push(x, z, r_ax.at[0], to_xf)
    a_push(x, z, r_ax.at[1], to_xb)
    a_start(0)
    b_push(x, z, r_bx.at[0, 0], to_xf)
    b_push(x, z, r_bx.at[1, 0], to_xb)
    load_amps.wait()

    def arrange(j, _):
        for b in range(BLOCKS):
            block = whole[pl.ds(SHARE * BLOCKS * j + b, SHARE, stride=BLOCKS), :]
            col = 128 * b % HALF
            sent[128 * b // HALF][j, :, col : col + 128] = block
        return 0

    lax.fori_loop(0, V, arrange, 0)
    for h in range(2):
        spread[h][vir] = sent[h][vir]

    tile_a, tile_b = pairs[0, vir], pairs[1, vir]
    task = tasks[vir]
    cd_a, cd_b = pairs[0, task], pairs[1, task]
    sub = lax.broadcasted_iota(jnp.int32, (ROWS, 128), 0)
    for par in range(2):
        key = jnp.zeros((ROWS, 128), jnp.int32)
        for j in range(ROWS):
            key = jnp.where(sub == j, irr[tile_b, par * ROWS + j], key)
        col_key[par] = key
    lane = lax.broadcasted_iota(jnp.int32, (1, 128), 1)
    minor = jnp.zeros((1, 128), jnp.int32)
    for j in range(TILE):
        minor = jnp.where(lane % TILE == j, irr[cd_b, j], minor)
    for b in range(BLOCKS):
        major = jnp.zeros((1, 128), jnp.int32)
        for j in range(4):
            major = jnp.where(lane // TILE == j, irr[cd_a, 4 * b + j], major)
        cd_key[:, 128 * b : 128 * b + 128] = major ^ minor

    prepare(x, z, 0, BLOCKS)

    a_wait(xb, z, r_ax.at[0])
    a_push(xb, z, r_ax.at[2], to_xf)
    a_start(1)
    a_wait(xf, z, r_ax.at[1])
    a_start(2)
    b_wait(xb, z, r_bx.at[0, 0])
    b_push(xb, z, r_bx.at[2, 0], to_xf)
    @pl.when(jnp.logical_not(is_hub))
    def _():
        pl.semaphore_wait(barrier, 1)

    spread_half(0)
    spread_half(1)
    prepare(xb, z, 0, BLOCKS)
    stage_b(0)
    stage_a(0, 0)
    a_wait(xo, z, r_ax.at[2])
    a_start(3)
    b_wait(xf, z, r_bx.at[1, 0])
    prepare(xf, z, 0, BLOCKS)

    def gather_amps(h):
        many = spread[h].at[pl.ds(0, V - 1)]
        pltpu.make_async_copy(many, many, r_y2.at[h]).wait()
        value = abuf[h]
        high = value.astype(jnp.bfloat16)
        cols = slice(HALF * h, HALF * h + HALF)
        aa[:OCC, cols] = high
        aa[OCC:, cols] = (value - high.astype(jnp.float32)).astype(jnp.bfloat16)

    def multiply(xx):
        span = Z * ROWS
        rows = pl.ds(pl.multiple_of(xx * span, span), span)
        right = aa[...]
        dims = (((1,), (1,)), ((), ()))
        part = lax.dot_general(ehi[rows, :], right, dims, preferred_element_type=jnp.float32)
        part += lax.dot_general(elo[rows, :], right, dims, preferred_element_type=jnp.float32)
        ladder = part[:, :OCC] + part[:, OCC:]
        for b in range(span // 128):
            here = pl.ds(xx * (span // 128) + b, OCC, stride=BLOCKS)
            out[here, :] = base[here, :] + ladder[128 * b : 128 * b + 128].T

    def later_a(t):
        stage_a(t, 1)
        stage_a(t, 2)
        settle_a(t, 0)

    def last_a(t):
        stage_a(t, 3)
        settle_b(t)
        settle_a(t, 1)
        settle_a(t, 2)

    later_a(0)
    stage_b(1)
    stage_a(1, 0)
    pass_on(0)
    last_a(0)
    b_wait(xo, z, r_bx.at[2, 0])
    prepare(xo, z, 0, BLOCKS)
    later_a(1)
    return_half(0)
    stage_b(2)
    stage_a(2, 0)
    pass_on(1)
    last_a(1)
    settle_a(0, 3)
    near(0)
    return_half(1)
    later_a(2)
    stage_b(3)
    stage_a(3, 0)
    pass_on(2)
    last_a(2)
    settle_a(1, 3)
    far(0)
    near(1)
    later_a(3)
    pass_on(3)
    last_a(3)
    settle_a(2, 3)
    far(1)
    near(2)
    settle_a(3, 3)
    far(2)
    gather_amps(0)
    gather_amps(1)
    load_resid.wait()
    multiply(x)
    near(3)
    multiply(xb)
    multiply(xf)
    far(3)
    multiply(xo)

    a_all = raw.at[pl.ds(0, SHARDS - 1), :, pl.ds(0, WA)]
    pltpu.make_async_copy(a_all, a_all, s_a.at[0]).wait()
    b_all = raw.at[pl.ds(0, SHARDS - 1), :, pl.ds(WA, WB)]
    pltpu.make_async_copy(b_all, b_all, s_b.at[0]).wait()
    for phase in range(2):
        for h in range(2):
            many = spread[h].at[pl.ds(0, V - 1)]
            pltpu.make_async_copy(many, many, s_y.at[phase, h]).wait()


def solution(mesh):
    def shards(amps, resid, ints, tasks, pair_tiles, irreps):
        smem = pl.BlockSpec(memory_space=pltpu.SMEM)
        hbm = pl.BlockSpec(memory_space=pl.ANY)
        dma = pltpu.SemaphoreType.DMA
        f32, bf16 = jnp.float32, jnp.bfloat16
        flat = (OCC * BLOCKS, 128)
        total = pl.pallas_call(
            kernel,
            out_shape=jax.ShapeDtypeStruct(flat, f32),
            in_specs=[smem, smem, smem, hbm, hbm, hbm],
            out_specs=pl.BlockSpec(memory_space=pltpu.VMEM),
            scratch_shapes=[
                pltpu.VMEM((SHARDS, ROWS, COLS), f32),
                pltpu.VMEM((COLS, COLS), bf16),
                pltpu.VMEM((COLS, COLS), bf16),
                pltpu.VMEM(flat, f32),
                pltpu.VMEM((V, SHARE, HALF), f32),
                pltpu.VMEM((V, SHARE, HALF), f32),
                pltpu.VMEM((V, SHARE, HALF), f32),
                pltpu.VMEM((V, SHARE, HALF), f32),
                pltpu.VMEM((2, V, SHARE, HALF), f32),
                pltpu.VMEM((2, OCC, HALF), f32),
                pltpu.VMEM((2 * OCC, COLS), bf16),
                pltpu.VMEM(flat, f32),
                pltpu.VMEM((2, ROWS, 128), jnp.int32),
                pltpu.VMEM((1, COLS), jnp.int32),
                dma((3,)),
                dma((1,)),
                dma((1,)),
                dma((2, 2)),
                dma((3,)),
                dma((FWD, X)),
                dma((BWD, X)),
                dma((FWD,)),
                dma((BWD,)),
                dma((3, Z)),
                dma((2,)),
                dma((2,)),
            ],
            compiler_params=pltpu.CompilerParams(collective_id=0, has_side_effects=True),
            name="ladder",
        )(tasks, pair_tiles.T, irreps, amps.reshape(flat), resid.reshape(flat), ints.reshape(ROWS, COLS))
        return total.reshape(OCC, 1, COLS)

    in_specs = (P("occ", "vir", None), P("occ", "vir", None), P("vir", "occ", None), P(), P(), P())
    return jax.shard_map(
        shards, mesh=mesh, in_specs=in_specs, out_specs=P("occ", "vir", None), check_vma=False
    )
```

```python
import jax
import jax.numpy as jnp
from jax import lax
from jax.experimental import pallas as pl
from jax.experimental.pallas import tpu as pltpu
from jax.sharding import PartitionSpec as P

MESH = pl.DeviceIdType.MESH
X, Z, V = 4, 16, 16
SHARDS = X * Z
ROWS = 16
TILE = 32
COLS = 1024
BLOCKS = COLS // 128
NA = 2
WA = NA * 128
WB = COLS - WA
OCC = 128
SHARE = OCC // V
HALF = COLS // 2
FWD, BWD = Z // 2, Z // 2 - 1
LAST = FWD // 2 - 1
HUB = V // 2


def kernel(
    tasks, pairs, irr, amps, resid, ints, out,
    raw, ehi, elo, whole, sent0, sent1, spread0, spread1, picked, abuf, aa, base, col_key, cd_key,
    s_loc, s_a, s_b, s_y, r_ax, r_af, r_ab, r_bf, r_bb, r_bx, r_y1, r_y2,
):
    occ, vir = lax.axis_index("occ"), lax.axis_index("vir")
    x, z = occ // Z, occ % Z
    sign = 1 - 2 * (vir % 2)
    xf, xb = (x + sign + X) % X, (x - sign + X) % X
    xo = (x + 2) % X
    zf, zb = (z + sign + Z) % Z, (z - sign + Z) % Z
    to_xf, to_xb = (xf * Z + z, vir), (xb * Z + z, vir)
    to_zf, to_zb = (x * Z + zf, vir), (x * Z + zb, vir)
    to_xo = (xo * Z + z, vir)
    to_zf2 = (x * Z + (z + 2 * sign + Z) % Z, vir)
    to_zb2 = (x * Z + (z - 2 * sign + Z) % Z, vir)

    sent, spread = (sent0, sent1), (spread0, spread1)
    load_amps = pltpu.make_async_copy(amps, whole, s_loc.at[1])
    load_amps.start()
    load_ints = pltpu.make_async_copy(ints, raw.at[occ], s_loc.at[0])
    load_ints.start()
    load_resid = pltpu.make_async_copy(resid, base, s_loc.at[2])
    load_resid.start()

    barrier = pltpu.get_barrier_semaphore()
    near_by = (to_xf, to_xb, to_xo, to_zf, to_zb, to_zf2, to_zb2)
    for who in near_by:
        pl.semaphore_signal(barrier, inc=1, device_id=who, device_id_type=MESH)

    is_hub = vir == HUB

    @pl.when(is_hub)
    def _():
        pl.semaphore_wait(barrier, len(near_by) + V - 1)

        def tell(m, _):
            peer = (occ, (vir + m) % V)
            pl.semaphore_signal(barrier, inc=1, device_id=peer, device_id_type=MESH)
            return 0

        lax.fori_loop(1, V, tell, 0)

    @pl.when(jnp.logical_not(is_hub))
    def _():
        pl.semaphore_wait(barrier, len(near_by))
        pl.semaphore_signal(barrier, inc=1, device_id=(occ, HUB), device_id_type=MESH)

    load_ints.wait()

    def peer_at(i):
        return (vir + V // 2 + ((i + 1) // 2) * (1 - 2 * (i % 2)) + V) % V

    def spread_half(h):
        def send(i, _):
            peer = peer_at(i)
            pltpu.make_async_remote_copy(
                sent[h].at[peer], spread[h].at[vir],
                s_y.at[0, h], r_y1.at[h], device_id=(occ, peer), device_id_type=MESH,
            ).start()
            return 0

        lax.fori_loop(0, V - 1, send, 0)

    own_rows = pl.ds(pl.multiple_of(SHARE * vir, SHARE), SHARE)

    def return_half(h):
        many = spread[h].at[pl.ds(0, V - 1)]
        pltpu.make_async_copy(many, many, r_y1.at[h]).wait()
        for k in range(V):
            picked[h, k] = spread[h][tasks[k]]
        abuf[h, own_rows] = picked[h, vir]

        def send(i, _):
            peer = peer_at(i)
            pltpu.make_async_remote_copy(
                picked.at[h, peer], abuf.at[h, own_rows],
                s_y.at[1, h], r_y2.at[h], device_id=(occ, peer), device_id_type=MESH,
            ).start()
            return 0

        lax.fori_loop(0, V - 1, send, 0)

    def a_part(xx, zz):
        return raw.at[xx * Z + zz, :, pl.ds(0, WA)]

    def b_part(xx, zz):
        return raw.at[xx * Z + zz, :, pl.ds(WA, WB)]

    def push(part, send_sem, recv_sem, who):
        return pltpu.make_async_remote_copy(
            part, part, send_sem, recv_sem, device_id=who, device_id_type=MESH
        )

    def a_push(xx, zz, recv_sem, who):
        push(a_part(xx, zz), s_a.at[0], recv_sem, who).start()

    def b_push(xx, zz, recv_sem, who):
        push(b_part(xx, zz), s_b.at[0], recv_sem, who).start()

    def a_wait(xx, zz, recv_sem):
        push(a_part(xx, zz), s_a.at[0], recv_sem, to_xf).wait_recv()

    def b_wait(xx, zz, recv_sem):
        push(b_part(xx, zz), s_b.at[0], recv_sem, to_xf).wait_recv()

    xs = (x, xb, xf, xo)

    def prepare(xx, zz, first, last):
        shard = xx * Z + zz
        key = col_key[shard % 2] ^ irr[tile_a, shard // 2]
        rows = pl.ds(pl.multiple_of(shard * ROWS, ROWS), ROWS)
        cols = slice(128 * first, 128 * last)
        keys = jnp.concatenate([key] * (last - first), axis=1)
        value = jnp.where(keys == cd_key[:, cols], raw[shard, :, cols], 0.0)
        high = value.astype(jnp.bfloat16)
        ehi[rows, cols] = high
        elo[rows, cols] = (value - high.astype(jnp.float32)).astype(jnp.bfloat16)

    ways = (
        (sign, FWD, r_af, r_bf, 0, to_zf, to_zf2),
        (-sign, BWD, r_ab, r_bb, FWD, to_zb, to_zb2),
    )

    def along(t):
        for d in (2 * t + 2, 2 * t + 1):
            for way in ways:
                if d <= way[1]:
                    yield d, (z - way[0] * d + Z) % Z, way

    def a_relay(i, d, zz, way):
        _, reach, r_a, _, _, to1, to2 = way
        if d + 2 <= reach:
            a_push(xs[i], zz, r_a.at[d + 1, i], to2)
        if d + 1 <= reach:
            a_push(xs[i], zz, r_a.at[d, i], to1)

    def b_relay(d, zz, way):
        _, reach, _, r_b, _, to1, to2 = way
        if d + 2 <= reach:
            b_push(x, zz, r_b.at[d + 1], to2)
        if d + 1 <= reach:
            b_push(x, zz, r_b.at[d], to1)

    def a_start(i):
        for way in ways:
            a_relay(i, 0, z, way)

    def stage_b(t):
        for d, zz, way in along(t):
            b_wait(x, zz, way[3].at[d - 1])
            if d % 2 == 0:
                b_relay(d, zz, way)
            b_push(x, zz, r_bx.at[0, way[4] + d], to_xf)
            b_push(x, zz, r_bx.at[1, way[4] + d], to_xb)
            if t == LAST:
                b_push(x, zz, r_bx.at[2, way[4] + d], to_xo)

    def stage_a(t, i):
        for d, zz, way in along(t):
            if d % 2 == 0:
                a_wait(xs[i], zz, way[2].at[d - 1, i])
                a_relay(i, d, zz, way)

    def settle_a(t, i):
        for d, zz, way in along(t):
            if d % 2 == 1:
                a_wait(xs[i], zz, way[2].at[d - 1, i])
            prepare(xs[i], zz, 0, NA)

    def settle_b(t):
        for d, zz, way in along(t):
            prepare(x, zz, NA, BLOCKS)

    def pass_on(t):
        for d, zz, way in along(t):
            q = way[4] + d
            if d % 2 == 0:
                b_wait(xb, zz, r_bx.at[0, q])
                if t < LAST:
                    b_push(xb, zz, r_bx.at[2, q], to_xf)
            else:
                b_wait(xf, zz, r_bx.at[1, q])
                if t < LAST:
                    b_push(xf, zz, r_bx.at[2, q], to_xb)

    def near(t):
        for d, zz, way in along(t):
            q = way[4] + d
            if d % 2 == 0:
                b_wait(xf, zz, r_bx.at[1, q])
            else:
                b_wait(xb, zz, r_bx.at[0, q])
            prepare(xb, zz, NA, BLOCKS)
            prepare(xf, zz, NA, BLOCKS)

    def far(t):
        for d, zz, way in along(t):
            q = way[4] + d
            b_wait(xo, zz, r_bx.at[2, q])
            prepare(xo, zz, NA, BLOCKS)

    for way in ways:
        b_relay(0, z, way)
    a_push(x, z, r_ax.at[0], to_xf)
    a_push(x, z, r_ax.at[1], to_xb)
    a_push(x, z, r_ax.at[2], to_xo)
    a_start(0)
    b_push(x, z, r_bx.at[0, 0], to_xf)
    b_push(x, z, r_bx.at[1, 0], to_xb)
    load_amps.wait()

    def arrange(j, _):
        for b in range(BLOCKS):
            block = whole[pl.ds(SHARE * BLOCKS * j + b, SHARE, stride=BLOCKS), :]
            col = 128 * b % HALF
            sent[128 * b // HALF][j, :, col : col + 128] = block
        return 0

    lax.fori_loop(0, V, arrange, 0)
    for h in range(2):
        spread[h][vir] = sent[h][vir]

    tile_a, tile_b = pairs[0, vir], pairs[1, vir]
    task = tasks[vir]
    cd_a, cd_b = pairs[0, task], pairs[1, task]
    sub = lax.broadcasted_iota(jnp.int32, (ROWS, 128), 0)
    for par in range(2):
        key = jnp.zeros((ROWS, 128), jnp.int32)
        for j in range(ROWS):
            key = jnp.where(sub == j, irr[tile_b, par * ROWS + j], key)
        col_key[par] = key
    lane = lax.broadcasted_iota(jnp.int32, (1, 128), 1)
    minor = jnp.zeros((1, 128), jnp.int32)
    for j in range(TILE):
        minor = jnp.where(lane % TILE == j, irr[cd_b, j], minor)
    for b in range(BLOCKS):
        major = jnp.zeros((1, 128), jnp.int32)
        for j in range(4):
            major = jnp.where(lane // TILE == j, irr[cd_a, 4 * b + j], major)
        cd_key[:, 128 * b : 128 * b + 128] = major ^ minor

    prepare(x, z, 0, BLOCKS)

    a_wait(xb, z, r_ax.at[0])
    a_start(1)
    a_wait(xf, z, r_ax.at[1])
    a_start(2)
    b_wait(xb, z, r_bx.at[0, 0])
    b_push(xb, z, r_bx.at[2, 0], to_xf)
    @pl.when(jnp.logical_not(is_hub))
    def _():
        pl.semaphore_wait(barrier, 1)

    spread_half(0)
    spread_half(1)
    prepare(xb, z, 0, BLOCKS)
    stage_b(0)
    stage_a(0, 0)
    a_wait(xo, z, r_ax.at[2])
    a_start(3)
    b_wait(xf, z, r_bx.at[1, 0])
    prepare(xf, z, 0, BLOCKS)

    def gather_amps(h):
        many = spread[h].at[pl.ds(0, V - 1)]
        pltpu.make_async_copy(many, many, r_y2.at[h]).wait()
        value = abuf[h]
        high = value.astype(jnp.bfloat16)
        cols = slice(HALF * h, HALF * h + HALF)
        aa[:OCC, cols] = high
        aa[OCC:, cols] = (value - high.astype(jnp.float32)).astype(jnp.bfloat16)

    def multiply(xx):
        span = Z * ROWS
        rows = pl.ds(pl.multiple_of(xx * span, span), span)
        right = aa[...]
        dims = (((1,), (1,)), ((), ()))
        part = lax.dot_general(ehi[rows, :], right, dims, preferred_element_type=jnp.float32)
        part += lax.dot_general(elo[rows, :], right, dims, preferred_element_type=jnp.float32)
        ladder = part[:, :OCC] + part[:, OCC:]
        for b in range(span // 128):
            here = pl.ds(xx * (span // 128) + b, OCC, stride=BLOCKS)
            out[here, :] = base[here, :] + ladder[128 * b : 128 * b + 128].T

    def later_a(t):
        stage_a(t, 1)
        stage_a(t, 2)
        settle_a(t, 0)

    def last_a(t):
        stage_a(t, 3)
        settle_b(t)
        settle_a(t, 1)
        settle_a(t, 2)

    later_a(0)
    stage_b(1)
    stage_a(1, 0)
    pass_on(0)
    last_a(0)
    b_wait(xo, z, r_bx.at[2, 0])
    prepare(xo, z, 0, BLOCKS)
    later_a(1)
    return_half(0)
    stage_b(2)
    stage_a(2, 0)
    pass_on(1)
    last_a(1)
    settle_a(0, 3)
    near(0)
    return_half(1)
    later_a(2)
    stage_b(3)
    stage_a(3, 0)
    pass_on(2)
    last_a(2)
    settle_a(1, 3)
    far(0)
    near(1)
    later_a(3)
    pass_on(3)
    last_a(3)
    settle_a(2, 3)
    far(1)
    near(2)
    settle_a(3, 3)
    far(2)
    gather_amps(0)
    gather_amps(1)
    load_resid.wait()
    multiply(x)
    near(3)
    multiply(xb)
    multiply(xf)
    far(3)
    multiply(xo)

    a_all = raw.at[pl.ds(0, SHARDS - 1), :, pl.ds(0, WA)]
    pltpu.make_async_copy(a_all, a_all, s_a.at[0]).wait()
    b_all = raw.at[pl.ds(0, SHARDS - 1), :, pl.ds(WA, WB)]
    pltpu.make_async_copy(b_all, b_all, s_b.at[0]).wait()
    for phase in range(2):
        for h in range(2):
            many = spread[h].at[pl.ds(0, V - 1)]
            pltpu.make_async_copy(many, many, s_y.at[phase, h]).wait()


def solution(mesh):
    def shards(amps, resid, ints, tasks, pair_tiles, irreps):
        smem = pl.BlockSpec(memory_space=pltpu.SMEM)
        hbm = pl.BlockSpec(memory_space=pl.ANY)
        dma = pltpu.SemaphoreType.DMA
        f32, bf16 = jnp.float32, jnp.bfloat16
        flat = (OCC * BLOCKS, 128)
        total = pl.pallas_call(
            kernel,
            out_shape=jax.ShapeDtypeStruct(flat, f32),
            in_specs=[smem, smem, smem, hbm, hbm, hbm],
            out_specs=pl.BlockSpec(memory_space=pltpu.VMEM),
            scratch_shapes=[
                pltpu.VMEM((SHARDS, ROWS, COLS), f32),
                pltpu.VMEM((COLS, COLS), bf16),
                pltpu.VMEM((COLS, COLS), bf16),
                pltpu.VMEM(flat, f32),
                pltpu.VMEM((V, SHARE, HALF), f32),
                pltpu.VMEM((V, SHARE, HALF), f32),
                pltpu.VMEM((V, SHARE, HALF), f32),
                pltpu.VMEM((V, SHARE, HALF), f32),
                pltpu.VMEM((2, V, SHARE, HALF), f32),
                pltpu.VMEM((2, OCC, HALF), f32),
                pltpu.VMEM((2 * OCC, COLS), bf16),
                pltpu.VMEM(flat, f32),
                pltpu.VMEM((2, ROWS, 128), jnp.int32),
                pltpu.VMEM((1, COLS), jnp.int32),
                dma((3,)),
                dma((1,)),
                dma((1,)),
                dma((2, 2)),
                dma((3,)),
                dma((FWD, X)),
                dma((BWD, X)),
                dma((FWD,)),
                dma((BWD,)),
                dma((3, Z)),
                dma((2,)),
                dma((2,)),
            ],
            compiler_params=pltpu.CompilerParams(collective_id=0, has_side_effects=True),
            name="ladder",
        )(tasks, pair_tiles.T, irreps, amps.reshape(flat), resid.reshape(flat), ints.reshape(ROWS, COLS))
        return total.reshape(OCC, 1, COLS)

    in_specs = (P("occ", "vir", None), P("occ", "vir", None), P("vir", "occ", None), P(), P(), P())
    return jax.shard_map(
        shards, mesh=mesh, in_specs=in_specs, out_specs=P("occ", "vir", None), check_vma=False
    )
```
